32 devices in a mesh: dp: 4 (over x, core), row: 4 (over z), col: 2 (over y).
Axes of the slice: x: 2, y: 2, z: 4, core: 2. Of those that a mesh axis runs over, the one named last changes fastest.
Arguments:
- tokens: bfloat16 [4096, 4096], P(('dp', 'col'), 'row'), may hold values from -6 to 6
- cotangent: bfloat16 [4096, 4096], P(('dp', 'col'), 'row'), may hold values from -6 to 6
- gate_pre: bfloat16 [4096, 14336], P(('dp', 'row'), 'col'), may hold values from -6 to 6
- up_pre: bfloat16 [4096, 14336], P(('dp', 'row'), 'col'), may hold values from -6 to 6
- w_gate: bfloat16 [14336, 4096], P('col', 'row'), may hold values from -0.09375 to 0.09375
- w_up: bfloat16 [14336, 4096], P('col', 'row'), may hold values from -0.09375 to 0.09375
- w_down: bfloat16 [4096, 14336], P('row', 'col'), may hold values from -0.046875 to 0.046875
Outputs:
- d_tokens: bfloat16 [4096, 4096], P(('dp', 'col'), 'row')
- grad_gate: float32 [14336, 4096], P(('col', 'dp'), 'row')
- grad_up: float32 [14336, 4096], P(('col', 'dp'), 'row')
- grad_down: float32 [4096, 14336], P(('row', 'dp'), 'col')
The draws below stay inside these ranges and needn't reach their ends.
All inputs are finite; a program needn't handle non-finite values.
Results may differ from the reference program's by a relative error of at most 0.02.
Values may be sent and summed in bfloat16 or wider, within the bound.
A program may use at most 256 MiB of HBM per device.

```python
import jax
import jax.numpy as jnp
from jax import lax

D = 4096
FF = 14336
TOKENS = 4096
N_ROW = 4


def strengthened(array, rng, source, target, shards_of, factor):
    def block_of(axis_at):
        return (jnp.arange(array.shape[axis_at]) // (array.shape[axis_at] // shards_of)).reshape((-1,) + (1,) * (array.ndim - 1 - axis_at))

    near = jax.random.permutation(rng, shards_of)[block_of(target)]
    far = (block_of(target) + shards_of // 2) % shards_of
    return jnp.where((block_of(source) == near) | (block_of(source) == far), factor * array, array)


def levels(key, shape, pieces, low, largest):
    gain = 1.0
    for position, blocks in pieces:
        steps = jax.random.uniform(jax.random.fold_in(jax.random.fold_in(key, 6), position), (blocks,), jnp.float32, low / len(pieces), largest / len(pieces))
        gain = gain * jnp.repeat(jnp.exp(steps), shape[position] // blocks).reshape((-1,) + (1,) * (len(shape) - 1 - position))
    return gain


def noise(rng, shape, spread, limit, shards=(), dtype=jnp.bfloat16):
    values = spread * jax.random.normal(rng, shape, jnp.float32)
    if shards:
        values = values * levels(rng, shape, shards, -0.22, 0.18)
    return jnp.clip(values, -limit, limit).astype(dtype)


def bell_draw_with(own_key, extent, width, most, shards, heavy, kind=jnp.bfloat16):
    drawn = width * jax.random.normal(own_key, extent, jnp.float32)
    if shards:
        drawn = drawn * levels(own_key, extent, shards, -0.22, 0.18)
    return jnp.clip(strengthened(drawn, jax.random.fold_in(own_key, 3), *heavy), -most, most).astype(kind)


def setup_inputs(seed: int = 0) -> dict:
    seeds = jax.random.split(jax.random.key(seed), 8)
    return {
        "tokens": noise(seeds[0], (TOKENS, D), 1.0, 6.0, ((0, 8), (1, 4))),
        "cotangent": bell_draw_with(seeds[1], (TOKENS, D), 1.0, 6.0, ((0, 8), (1, 4)), (0, 1, 8, 2.0)),
        "gate_pre": noise(seeds[2], (TOKENS, FF), 1.5, 6.0, ((0, 16), (1, 2))),
        "up_pre": noise(seeds[3], (TOKENS, FF), 1.0, 6.0, ((0, 16), (1, 2))),
        "w_gate": noise(seeds[4], (FF, D), D ** -0.5, 0.09375, ((0, 2), (1, 4))),
        "w_up": noise(seeds[5], (FF, D), D ** -0.5, 0.09375, ((0, 2), (1, 4))),
        "w_down": noise(seeds[6], (D, FF), FF ** -0.5, 0.046875, ((0, 4), (1, 2))),
    }


def reference(tokens, cotangent, gate_pre, up_pre, w_gate, w_up, w_down):
    block_width = D // N_ROW
    cot_blocks = jnp.transpose(cotangent.reshape(TOKENS, N_ROW, block_width), (1, 0, 2))
    down_blocks = w_down.reshape(N_ROW, block_width, FF)

    def accumulate(running, block_pair):
        cot_block, down_block = block_pair
        product = jnp.dot(cot_block, down_block, preferred_element_type=jnp.float32)
        rounded = lax.optimization_barrier(product.astype(jnp.bfloat16))
        return running + rounded.astype(jnp.float32), None

    hidden_grad, _ = lax.scan(accumulate, jnp.zeros((TOKENS, FF), jnp.float32), (cot_blocks, down_blocks))
    gate_value = gate_pre.astype(jnp.float32)
    up_value = up_pre.astype(jnp.float32)
    sigmoid_gate = jax.nn.sigmoid(gate_value)
    hidden = (gate_value * sigmoid_gate * up_value).astype(jnp.bfloat16)
    gate_grad = (hidden_grad * up_value * sigmoid_gate * (1.0 + gate_value * (1.0 - sigmoid_gate))).astype(jnp.bfloat16)
    up_grad = (hidden_grad * gate_value * sigmoid_gate).astype(jnp.bfloat16)
    d_tokens = (jnp.dot(gate_grad, w_gate, preferred_element_type=jnp.float32) + jnp.dot(up_grad, w_up, preferred_element_type=jnp.float32)).astype(jnp.bfloat16)
    grad_gate = jnp.dot(gate_grad.T, tokens, preferred_element_type=jnp.float32)
    grad_up = jnp.dot(up_grad.T, tokens, preferred_element_type=jnp.float32)
    grad_down = jnp.dot(cotangent.T, hidden, preferred_element_type=jnp.float32)
    return (d_tokens, grad_gate, grad_up, grad_down)
```

```python
import jax
import jax.numpy as jnp
from jax import lax
from jax.sharding import PartitionSpec as P


def contract_tokens(left, right):
    return lax.dot_general(
        left, right, (((0,), (0,)), ((), ())), preferred_element_type=jnp.float32
    )


def add_rounded(left, right):
    return (left.astype(jnp.float32) + right.astype(jnp.float32)).astype(jnp.bfloat16)


def gather_rows(block, axis):
    count = lax.axis_size(axis)
    if count != 2:
        return lax.all_gather(block, axis, axis=0, tiled=True)
    other = lax.ppermute(block, axis, [(0, 1), (1, 0)])
    first = lax.axis_index(axis) == 0
    return jnp.concatenate([jnp.where(first, block, other), jnp.where(first, other, block)], axis=0)


def line_reduce_scatter(partial, axis):
    count = lax.axis_size(axis)
    size = partial.shape[0] // count
    me = lax.axis_index(axis)

    def block(index):
        start = jnp.clip(index, 0, count - 1) * size
        return lax.dynamic_slice_in_dim(partial, start, size, axis=0)

    right = left = None
    for step in range(count - 1):
        up_block = block(count - 1 - step + me)
        down_block = block(step - (count - 1 - me))
        if step:
            up_block, down_block = add_rounded(up_block, right), add_rounded(down_block, left)
        senders = range(min(step, count - 2) + 1)
        right = lax.ppermute(up_block, axis, [(i, i + 1) for i in senders])
        left = lax.ppermute(down_block, axis, [(count - 1 - i, count - 2 - i) for i in senders])
    own = block(me).astype(jnp.float32)
    return own + right.astype(jnp.float32) + left.astype(jnp.float32)


def halving_reduce_scatter(partial, axis):
    count = lax.axis_size(axis)
    if count & (count - 1):
        return lax.psum_scatter(partial, axis, scatter_dimension=0, tiled=True).astype(jnp.float32)
    me = lax.axis_index(axis)
    total = partial.reshape((count, partial.shape[0] // count) + partial.shape[1:])
    bit = 1
    while bit < count:
        mine = (me // bit) % 2
        pairs = total.reshape((total.shape[0] // 2, 2) + total.shape[1:])
        keep = lax.dynamic_index_in_dim(pairs, mine, axis=1, keepdims=False)
        send = lax.dynamic_index_in_dim(pairs, 1 - mine, axis=1, keepdims=False)
        got = lax.ppermute(send, axis, [(i, i ^ bit) for i in range(count)])
        bit *= 2
        if bit < count:
            total = add_rounded(keep, got)
        else:
            total = keep.astype(jnp.float32) + got.astype(jnp.float32)
    return total.reshape(total.shape[1:])


def local(tokens, cotangent, gate_pre, up_pre, w_gate, w_up, w_down):
    owners = lax.axis_size("dp")
    hidden_units = gate_pre.shape[1]
    gate_value = gate_pre.astype(jnp.float32)
    up_value = up_pre.astype(jnp.float32)
    sigmoid_gate = jax.nn.sigmoid(gate_value)
    hidden = (gate_value * sigmoid_gate * up_value).astype(jnp.bfloat16)

    cot_cols = gather_rows(cotangent, "col")
    cot_cols, hidden = lax.optimization_barrier((cot_cols, hidden))
    hidden_all = lax.all_gather(hidden, "row", axis=0, tiled=True)
    tok_cols = gather_rows(tokens, "col")

    halves = 2 if hidden_units % 256 == 0 else 1
    width = hidden_units // halves
    sums = []
    for h in range(halves):
        part = jnp.dot(
            cot_cols, w_down[:, h * width : (h + 1) * width], preferred_element_type=jnp.float32
        ).astype(jnp.bfloat16)
        sums.append(line_reduce_scatter(part, "row"))
    hidden_grad = jnp.concatenate(sums, axis=1)

    hidden_grad, gate_pre, up_pre = lax.optimization_barrier((hidden_grad, gate_pre, up_pre))
    gate_value = gate_pre.astype(jnp.float32)
    up_value = up_pre.astype(jnp.float32)
    sigmoid_gate = jax.nn.sigmoid(gate_value)
    gate_grad = (
        hidden_grad * up_value * sigmoid_gate * (1.0 + gate_value * (1.0 - sigmoid_gate))
    ).astype(jnp.bfloat16)
    up_grad = (hidden_grad * gate_value * sigmoid_gate).astype(jnp.bfloat16)

    gate_grad, hidden_all = lax.optimization_barrier((gate_grad, hidden_all))
    gate_all = lax.all_gather(gate_grad, "row", axis=0, tiled=True)
    grad_down = halving_reduce_scatter(
        contract_tokens(cot_cols, hidden_all).astype(jnp.bfloat16), "dp"
    )
    owned = hidden_units // owners
    chunks = 2 if owned % 256 == 0 else 1
    piece = owned // chunks
    up_grads = []
    gathered, settled = gate_all, grad_down
    weights = w_gate
    grad_gate = token_sum = None
    for k in range(chunks):
        starts = [q * owned + k * piece for q in range(owners)]
        up_part = jnp.concatenate([up_grad[:, s : s + piece] for s in starts], axis=1)
        up_part, gathered, settled = lax.optimization_barrier((up_part, gathered, settled))
        if k == 0:
            grad_down = settled
        elif k == 1:
            grad_gate = settled
        else:
            up_grads[-1] = settled
        up_all = lax.all_gather(up_part, "row", axis=0, tiled=True)
        settled = halving_reduce_scatter(
            contract_tokens(gathered, tok_cols).astype(jnp.bfloat16), "dp"
        )
        if k == 0:
            grad_gate = settled
        else:
            up_grads.append(settled)
        product = jnp.dot(gathered, weights, preferred_element_type=jnp.float32)
        token_sum = product if token_sum is None else token_sum + product
        weights = jnp.concatenate([w_up[s : s + piece] for s in starts], axis=0)
        gathered = up_all
    product = jnp.dot(gathered, weights, preferred_element_type=jnp.float32)
    up_grads.append(
        halving_reduce_scatter(contract_tokens(gathered, tok_cols).astype(jnp.bfloat16), "dp")
    )
    token_sum = token_sum + product
    grad_up = jnp.concatenate(up_grads, axis=0)
    d_tokens = halving_reduce_scatter(token_sum.astype(jnp.bfloat16), "col").astype(jnp.bfloat16)
    return (d_tokens, grad_gate, grad_up, grad_down)


def solution(mesh):
    placed = (
        P(("dp", "col"), "row"),
        P(("dp", "col"), "row"),
        P(("dp", "row"), "col"),
        P(("dp", "row"), "col"),
        P("col", "row"),
        P("col", "row"),
        P("row", "col"),
    )
    return jax.shard_map(
        local,
        mesh=mesh,
        in_specs=placed,
        out_specs=(
            P(("dp", "col"), "row"),
            P(("col", "dp"), "row"),
            P(("col", "dp"), "row"),
            P(("row", "dp"), "col"),
        ),
        check_vma=False,
    )
```
